256 devices in a mesh: row: 64 (over y, z, core), col: 4 (over x).
Axes of the slice: x: 4, y: 4, z: 8, core: 2. Of those that a mesh axis runs over, the one named last changes fastest.
Arguments:
- leaf_grad: bfloat16 [256, 32, 1024], P('row', None, 'col'), may hold values from -6 to 6
- leaf_inv: bfloat16 [256, 1024, 1024], P('row', 'col'), as said below
- leaf_cpl: bfloat16 [256, 1024, 512], P('row', 'col'), may hold values from -0.046875 to 0.046875
- leaf_size: int32 [256], P('row'), may hold values from 256 to 1024, as said below
- leaf_parent: int32 [256], P('row'), may hold values from 0 to 3
- leaf_map: int32 [256, 512], P('row'), may hold values from 0 to 2047
- mid_grad: bfloat16 [32, 4, 2048], P(None, 'col', 'row'), may hold values from -6 to 6
- mid_inv: bfloat16 [4, 2048, 2048], P('col', 'row'), as said below
- mid_cpl: bfloat16 [4, 2048, 512], P('col', 'row'), may hold values from -0.125 to 0.125
- mid_map: int32 [4, 512], replicated, may hold values from 0 to 2047
- root_grad: bfloat16 [32, 2048], P(None, 'row'), may hold values from -6 to 6
- root_inv: bfloat16 [2048, 2048], P('row'), as said below
Outputs:
- leaf_x: float32 [256, 32, 1024], P('row', None, 'col')
- mid_x: float32 [32, 4, 2048], P(None, 'col', 'row')
- root_x: float32 [32, 2048], P(None, 'row')
The draws below stay inside these ranges and needn't reach their ends.
Inputs may be any that keep to these rules, and one draw needn't show every extreme that they name: `leaf_size`: some leaf in every draw has 1024 live pivot columns. `leaf_map`: columns may repeat. `mid_map`: columns may repeat. `leaf_inv`: upper triangular; diagonal entries between 1 and 1.25, entries above the diagonal of scale 1024 ** -0.5. `mid_inv`: each front's block is upper triangular; diagonal entries between 1 and 1.25, entries above the diagonal of scale 2048 ** -0.5. `root_inv`: upper triangular; diagonal entries between 1 and 1.25, entries above the diagonal of scale 2048 ** -0.5.
All inputs are finite; a program needn't handle non-finite values.
Results may differ from the reference program's by a relative error of at most 0.012.
Values may be sent and summed in bfloat16 or wider, within the bound.
No kernel may reach another device: no remote copies, remote signals or barrier semaphores. Data moves between devices by JAX's collectives and lax.ppermute only.
A program may use at most 64 MiB of HBM per device.

```python
import math
import jax
import jax.numpy as jnp
from jax import lax

K = 32
P0 = 1024
C0 = 512
P1 = 2048
C1 = 512
P2 = 2048
LEAF_DEV = 4
NLEAF = 256
N_MID = 4
N_ROW = 64
N_COL = 4


def triangle_stack(key, count, order):
    upper_vals = jax.random.normal(key, (count, order, order), jnp.float32)
    diag_vals = 1.0 + 0.25 * jax.random.uniform(jax.random.fold_in(key, 3), (count, order, order), jnp.float32)
    row_ids = lax.broadcasted_iota(jnp.int32, (count, order, order), 1)
    col_ids = lax.broadcasted_iota(jnp.int32, (count, order, order), 2)
    scaled = upper_vals / math.sqrt(order)
    return jnp.where(col_ids > row_ids, scaled, jnp.where(col_ids == row_ids, diag_vals, 0.0))


def draw_leaf_inv(key, part):
    return triangle_stack(key, NLEAF, P0).astype(jnp.bfloat16)


def draw_mid_inv(key, part):
    return triangle_stack(key, N_MID, P1).astype(jnp.bfloat16)


def draw_root_inv(key, part):
    return triangle_stack(key, 1, P2)[0].astype(jnp.bfloat16)


def draw_leaf_size(key, part):
    counts = jax.random.randint(key, (NLEAF,), P0 // 4, P0 + 1)
    chosen = jax.random.randint(jax.random.fold_in(key, 7), (), 0, NLEAF)
    return counts.at[chosen].set(P0).astype(jnp.int32)


def place_ends(values, rng, low, largest):
    extent = values.shape
    spot = [jax.random.randint(jax.random.fold_in(rng, axis), (), 0, extent[axis]) for axis in range(len(extent))]
    values = values.at[tuple(spot)].set(low)
    longest = extent.index(max(extent))
    spot[longest] = (spot[longest] + 1) % extent[longest]
    return values.at[tuple(spot)].set(largest)


def steps_of(stream_key, shape, shards, low, top_value):
    factor_of, own = 1.0, jax.random.fold_in(stream_key, 6)
    for dim, parts in shards:
        draws = jnp.exp(jax.random.uniform(jax.random.fold_in(own, dim), (parts,), jnp.float32, low / len(shards), top_value / len(shards)))
        factor_of = factor_of * jnp.repeat(draws, shape[dim] // parts).reshape([-1 if axis == dim else 1 for axis in range(len(shape))])
    return factor_of


def scatter_about(key, extent, scale, reach, split=(), held_as=jnp.bfloat16):
    factor_of = steps_of(key, extent, split, -0.22, 0.18) if split else 1.0
    values = jax.random.normal(key, extent, jnp.float32) * scale * factor_of
    return jnp.minimum(jnp.maximum(values, -reach), reach).astype(held_as)


def setup_inputs(seed: int = 0) -> dict:
    streams_of = jax.random.split(jax.random.key(seed), 13)
    return {
        "leaf_grad": scatter_about(streams_of[0], (NLEAF, K, P0), 1.0, 6.0, ((0, 64), (2, 4))),
        "leaf_inv": draw_leaf_inv(jax.random.fold_in(streams_of[12], 71), 0),
        "leaf_cpl": scatter_about(streams_of[2], (NLEAF, P0, C0), (P0 * max(1, LEAF_DEV * N_ROW * C0 // (N_COL * P1))) ** -0.5, 0.046875, ((0, 64), (1, 4))),
        "leaf_size": draw_leaf_size(jax.random.fold_in(streams_of[12], 71), 0),
        "leaf_parent": place_ends(jax.random.randint(streams_of[4], (NLEAF,), 0, N_MID), jax.random.fold_in(streams_of[4], 1), 0, N_MID - 1).astype(jnp.int32),
        "leaf_map": place_ends(jax.random.randint(streams_of[5], (NLEAF, C0), 0, P1), jax.random.fold_in(streams_of[5], 1), 0, P1 - 1).astype(jnp.int32),
        "mid_grad": scatter_about(streams_of[6], (K, N_MID, P1), 1.0, 6.0, ((1, 4), (2, 64))),
        "mid_inv": draw_mid_inv(jax.random.fold_in(streams_of[12], 71), 0),
        "mid_cpl": scatter_about(streams_of[8], (N_MID, P1, C1), (P1 * max(1, N_MID * C1 // P2)) ** -0.5, 0.125, ((0, 4), (1, 64))),
        "mid_map": place_ends(jax.random.randint(streams_of[9], (N_MID, C1), 0, P2), jax.random.fold_in(streams_of[9], 1), 0, P2 - 1).astype(jnp.int32),
        "root_grad": scatter_about(streams_of[10], (K, P2), 1.0, 6.0, ((1, 64),)),
        "root_inv": draw_root_inv(jax.random.fold_in(streams_of[12], 71), 0),
    }


def rounded(values):
    return lax.optimization_barrier(values.astype(jnp.bfloat16))


def reference(leaf_grad, leaf_inv, leaf_cpl, leaf_size, leaf_parent, leaf_map, mid_grad, mid_inv, mid_cpl, mid_map, root_grad, root_inv):
    front = mid_inv.shape[1]
    nmiddle = mid_map.shape[0]
    columns = jnp.arange(P0)

    def leaf_forward(carry, items):
        grad, inverse, couple, size, parent, cmap = items
        mask = columns[None, :] < size
        solved = jnp.dot(grad.astype(jnp.float32), inverse.astype(jnp.float32), preferred_element_type=jnp.float32)
        solved = jnp.where(mask, solved, 0.0)
        share = jnp.dot(rounded(solved).astype(jnp.float32), couple.astype(jnp.float32), preferred_element_type=jnp.float32)
        carry = carry.at[:, parent * front + cmap].add(share)
        return carry, solved

    start = jnp.zeros((K, nmiddle * front), jnp.float32)
    contrib, leaf_y = lax.scan(leaf_forward, start, (leaf_grad, leaf_inv, leaf_cpl, leaf_size, leaf_parent, leaf_map))
    mid_hb = rounded(mid_grad.astype(jnp.float32) - contrib.reshape(K, nmiddle, front))
    inv_three = mid_inv.astype(jnp.float32)
    cpl_three = mid_cpl.astype(jnp.float32)
    mid_y = jnp.einsum('kpa,pab->kpb', mid_hb.astype(jnp.float32), inv_three)
    mid_u = jnp.einsum('kpa,pac->kpc', rounded(mid_y).astype(jnp.float32), cpl_three)
    root_total = jnp.zeros((K, P2), jnp.float32).at[:, mid_map.reshape(-1)].add(mid_u.reshape(K, nmiddle * C1))
    root_hb = rounded(root_grad.astype(jnp.float32) - root_total)
    root_f = root_inv.astype(jnp.float32)
    root_y = jnp.dot(root_hb.astype(jnp.float32), root_f, preferred_element_type=jnp.float32)
    root_x = jnp.dot(rounded(root_y).astype(jnp.float32), root_f.T, preferred_element_type=jnp.float32)
    root_xb = rounded(root_x).astype(jnp.float32)
    coupled = root_xb[:, mid_map]
    mid_w = mid_y - jnp.einsum('kpc,pbc->kpb', coupled, cpl_three)
    mid_x = jnp.einsum('kpa,pba->kpb', rounded(mid_w).astype(jnp.float32), inv_three)
    mid_xb = rounded(mid_x).astype(jnp.float32).reshape(K, nmiddle * front)

    def leaf_backward(items):
        solved, inverse, couple, size, parent, cmap = items
        mask = columns[None, :] < size
        picked = mid_xb[:, parent * front + cmap]
        resid = solved - jnp.dot(picked, couple.astype(jnp.float32).T, preferred_element_type=jnp.float32)
        resid = jnp.where(mask, resid, 0.0)
        return jnp.dot(rounded(resid).astype(jnp.float32), inverse.astype(jnp.float32).T, preferred_element_type=jnp.float32)

    leaf_x = lax.map(leaf_backward, (leaf_y, leaf_inv, leaf_cpl, leaf_size, leaf_parent, leaf_map))
    return leaf_x, mid_x, root_x
```

```python
import jax
import jax.numpy as jnp
from jax import lax
from jax.sharding import Mesh, PartitionSpec as P

BF = jnp.bfloat16
F32 = jnp.float32


def mm(a, b):
    return jnp.dot(a, b, preferred_element_type=F32)


def mm_t(a, b):
    return lax.dot_general(a, b, (((1,), (1,)), ((), ())), preferred_element_type=F32)


def a2a(v, axes):
    return lax.all_to_all(v, axes, 0, 0, tiled=True)


def spread(v, axes):
    n = lax.axis_size(axes)
    return lax.all_to_all(
        jnp.broadcast_to(v[None], (n,) + v.shape), axes, 0, 0, tiled=True
    )


def swap(v):
    return lax.ppermute(v, "c", [(0, 1), (1, 0)])


def half_sum(v, core):
    k = v.shape[-2] // 2
    lo, hi = v[..., :k, :], v[..., k:, :]
    mine = jnp.where(core == 0, lo, hi)
    theirs = jnp.where(core == 0, hi, lo).astype(BF)
    return mine + swap(theirs).astype(F32)


def both_halves(v, core):
    other = swap(v)
    lo = jnp.where(core == 0, v, other)
    hi = jnp.where(core == 0, other, v)
    return jnp.concatenate([lo, hi], axis=-2)


def to_tiles(v):
    k, n = v.shape
    return v.reshape(k // 8, 8, n // 128, 128).transpose(0, 2, 1, 3).reshape(-1, 8, 128)


def from_tiles(v, k, n):
    return v.reshape(k // 8, n // 128, 8, 128).transpose(0, 2, 1, 3).reshape(k, n)


def body(
    leaf_grad,
    leaf_inv,
    leaf_cpl,
    leaf_size,
    leaf_parent,
    leaf_map,
    mid_grad,
    mid_inv,
    mid_cpl,
    mid_map,
    root_grad,
    root_inv,
):
    ny, nz, nc, nx = (lax.axis_size(a) for a in ("y", "z", "c", "x"))
    iy, iz, ic, ix = (lax.axis_index(a) for a in ("y", "z", "c", "x"))
    nl, share, order = leaf_inv.shape
    nk = leaf_grad.shape[1]
    rows, front = mid_inv.shape[1:]
    ncpl = leaf_cpl.shape[2]
    nmid = mid_map.shape[0]
    parts = ny * nc
    width = front // parts

    def renumber(m):
        i = m % rows
        c = m // rows % nc
        z = m // (rows * nc) % nz
        y = m // (rows * nc * nz)
        return ((z * ny + y) * nc + c) * rows + i

    own = ((iz * ny + iy) * nc + ic) * rows

    with jax.named_scope("gather_inverses"):
        pm = mm(mid_grad[:, 0, :], mid_inv[0]).astype(BF)
        pr = mm(root_grad, root_inv).astype(BF)
        both = jnp.stack(
            [
                jnp.concatenate([mid_inv[0], pm], 0),
                jnp.concatenate([root_inv, pr], 0),
            ]
        )
        both = both.reshape(2, rows + nk, ny, nz, nc, rows)
        both = both.transpose(2, 4, 1, 0, 3, 5).reshape(parts, rows + nk, 2 * width)
        got = a2a(both, ("y", "c"))
        psum = jnp.sum(got[:, rows:].astype(F32), 0).astype(BF)
        mine = jnp.concatenate(
            [got[:, :rows].reshape(parts * rows, 2 * width), psum, mid_cpl[0]], 0
        )
        wide = lax.all_gather(mine, "z", axis=0)
        nr = parts * rows
        cols = wide[:, :nr].reshape(front, 2 * width)
        minv, rinv = cols[:, :width], cols[:, width:]
        pres = jnp.sum(wide[:, nr : nr + nk].astype(F32), 0)
        pre_m, pre_r = pres[:, :width], pres[:, width:]
        mcpl = wide[:, nr + nk :].reshape(width, ncpl)

    with jax.named_scope("leaf_forward"):
        live = (ix * share + lax.iota(jnp.int32, share))[None, :] < leaf_size[:, None]
        live = live[:, None, :]
        part = jnp.einsum(
            "lkp,lpxq->xlkq",
            leaf_grad,
            leaf_inv.reshape(nl, share, nx, share),
            preferred_element_type=F32,
        ).astype(BF)
        leaf_y = jnp.where(live, jnp.sum(a2a(part, "x").astype(F32), 0), 0.0)
        leaf_u = jnp.einsum(
            "lkp,lpc->klc", leaf_y.astype(BF), leaf_cpl, preferred_element_type=F32
        ).astype(BF)
    with jax.named_scope("leaf_spread"):
        target = renumber(leaf_map)
        hot = (target.reshape(-1)[:, None] == lax.iota(jnp.int32, front)[None, :]).astype(BF)
        parent_of = jnp.arange(nmid)[:, None] == leaf_parent[None, :]
        lhs = jnp.where(parent_of[:, None, :, None], leaf_u[None], 0).reshape(
            nmid * nk, nl * ncpl
        )
        placed = mm(lhs, hot).reshape(nmid, nk, front)
    with jax.named_scope("contrib_sum"):
        s = half_sum(placed, ic).astype(BF)
        s = jnp.sum(a2a(s, "x").astype(F32), 0).astype(BF)
        s = jnp.sum(a2a(to_tiles(s), ("y", "z")).reshape(ny * nz, 8, 128).astype(F32), 0)
        s = spread(s.astype(BF), ("y", "z"))
        contrib = both_halves(from_tiles(s.reshape(-1, 8, 128), nk // 2, front), ic)
    with jax.named_scope("mid_forward"):
        mid_y = pre_m - mm(contrib, minv)
        mid_u = half_sum(mm(mid_y.astype(BF), mcpl), ic).astype(BF)
        u = spread(mid_u, ("y", "x")).reshape(ny, nx, nk // 2, ncpl)
        u = both_halves(jnp.sum(u.astype(F32), 0).astype(BF), ic)
    with jax.named_scope("root"):
        rmap = renumber(mid_map)
        rhot = (rmap.reshape(-1)[:, None] == lax.iota(jnp.int32, front)[None, :]).astype(BF)
        total = mm(u.transpose(1, 0, 2).reshape(nk, nmid * ncpl), rhot).astype(BF)
        root_y = (pre_r - mm(total, rinv)).astype(BF)
        rx = half_sum(mm_t(root_y, rinv), ic).astype(BF)
        rx = jnp.sum(spread(rx, "y").reshape(ny, nk // 2, front).astype(F32), 0).astype(BF)
        root_x = both_halves(rx, ic)
    with jax.named_scope("mid_backward"):
        mymap = lax.dynamic_index_in_dim(rmap, ix, 0, keepdims=False)
        myhot = (mymap[:, None] == lax.iota(jnp.int32, front)[None, :]).astype(BF)
        coupled = mm_t(root_x, myhot).astype(BF)
        mid_w = (mid_y - mm_t(coupled, mcpl)).astype(BF)
        mx = half_sum(mm_t(mid_w, minv), ic).astype(BF)
        mx = spread(mx, ("y", "x")).reshape(ny, nx, nk // 2, front)
        mid_x = both_halves(jnp.sum(mx.astype(F32), 0).astype(BF), ic)
    with jax.named_scope("leaf_backward"):
        hot3 = hot.reshape(nl, ncpl, front)
        picked = jnp.einsum(
            "lkn,lcn->lkc", mid_x[leaf_parent], hot3, preferred_element_type=F32
        ).astype(BF)
        leaf_w = leaf_y - jnp.einsum(
            "lkc,lpc->lkp", picked, leaf_cpl, preferred_element_type=F32
        )
        leaf_w = jnp.where(live, leaf_w, 0.0).astype(BF)
        full = spread(leaf_w, "x").reshape(nx, nl, nk, share)
        leaf_x = jnp.einsum(
            "xlkq,lpxq->lkp",
            full,
            leaf_inv.reshape(nl, share, nx, share),
            preferred_element_type=F32,
        )
    out_m = lax.dynamic_slice(
        lax.dynamic_index_in_dim(mid_x, ix, 0, keepdims=False), (0, own), (nk, rows)
    )
    out_r = lax.dynamic_slice(root_x, (0, own), (nk, rows))
    return leaf_x, out_m.astype(F32)[:, None, :], out_r.astype(F32)


def solution(mesh):
    grid = Mesh(mesh.devices.reshape(4, 8, 2, 4), ("y", "z", "c", "x"))
    row = ("y", "z", "c")
    placed = (
        P(row, None, "x"),
        P(row, "x", None),
        P(row, "x", None),
        P(row),
        P(row),
        P(row, None),
        P(None, "x", row),
        P("x", row, None),
        P("x", row, None),
        P(),
        P(None, row),
        P(row, None),
    )
    return jax.shard_map(
        body,
        mesh=grid,
        in_specs=placed,
        out_specs=(P(row, None, "x"), P(None, "x", row), P(None, row)),
        check_vma=False,
    )
```

```python
import functools

import jax
import jax.numpy as jnp
from jax import lax
from jax.experimental import pallas as pl
from jax.experimental.pallas import tpu as pltpu
from jax.sharding import Mesh, PartitionSpec as P

BF = jnp.bfloat16
F32 = jnp.float32
VM = pl.BlockSpec(memory_space=pltpu.VMEM)
SM = pl.BlockSpec(memory_space=pltpu.SMEM)
PARAMS = pltpu.CompilerParams(vmem_limit_bytes=56 * 2**20)


def mm(a, b):
    return jnp.dot(a, b, preferred_element_type=F32)


def mm_t(a, b):
    return lax.dot_general(a, b, (((1,), (1,)), ((), ())), preferred_element_type=F32)


def a2a(v, axes):
    return lax.all_to_all(v, axes, 0, 0, tiled=True)


def spread(v, axes):
    n = lax.axis_size(axes)
    return a2a(jnp.broadcast_to(v[None], (n,) + v.shape), axes)


def swap(v):
    return lax.ppermute(v, "c", [(0, 1), (1, 0)])


def ahead(v, axis):
    n = lax.axis_size(axis)
    return [v] + [
        lax.ppermute(v, axis, [((i + k) % n, i) for i in range(n)]) for k in range(1, n)
    ]


def flip(v):
    n = v.shape[-1] // 2
    return jnp.concatenate([v[..., n:], v[..., :n]], -1)


def after(v, *first):
    return lax.optimization_barrier((v,) + first)[0]


def by_core(core, first, second):
    return jnp.where(core == 0, first, second), jnp.where(core == 0, second, first)


def root_pack_kernel(at, inv_ref, grad_ref, cpl_ref, out_ref, keep_ref):
    rows, nk = inv_ref.shape[0], grad_ref.shape[0]
    keep_ref[...] = inv_ref[...]
    out_ref[:rows, :] = inv_ref[...]
    out_ref[rows : rows + nk, :] = mm(grad_ref[...], inv_ref[...]).astype(BF)
    out_ref[rows + nk :, :] = cpl_ref[...]


def pack_kernel(nk, iy, inv_ref, g0, g1, g2, g3, out_ref):
    rows, front = inv_ref.shape
    got = (g0, g1, g2, g3)
    n = g0.shape[1]
    lane = lax.broadcasted_iota(jnp.int32, (rows, 128), 1) // 32
    for pair in range(front // 256):
        a = inv_ref[:, pair * 256 : pair * 256 + 128].astype(F32)
        b = inv_ref[:, pair * 256 + 128 : pair * 256 + 256].astype(F32)
        for c in range(2):
            if c == 0:
                parts = [a, pltpu.roll(a, 96, 1), pltpu.roll(b, 64, 1), pltpu.roll(b, 32, 1)]
            else:
                parts = [pltpu.roll(a, 96, 1), pltpu.roll(a, 64, 1), pltpu.roll(b, 32, 1), b]
            v = jnp.where(
                lane == 0,
                parts[0],
                jnp.where(lane == 1, parts[1], jnp.where(lane == 2, parts[2], parts[3])),
            )
            at = c * (front // 2) + pair * 128
            out_ref[:rows, at : at + 128] = v.astype(BF)
    for i, ref in enumerate(got):
        out_ref[2 * rows : 3 * rows, i * n : (i + 1) * n] = ref[:rows, :]
        s = lax.rem(iy[0] + i, len(got))
        for j in range(len(got)):

            @pl.when(s == j)
            def _():
                out_ref[rows : 2 * rows, j * n : (j + 1) * n] = ref[rows + nk :, :]

    pre = sum(ref[rows : rows + nk, :].astype(F32) for ref in got).astype(BF)
    step = nk // len(got)
    for i in range(len(got)):
        out_ref[3 * rows :, i * n : (i + 1) * n] = pre[i * step : (i + 1) * step, :]


def mid_kernel(core, h_ref, m0_ref, m1_ref, c0_ref, c1_ref, y_ref, u_ref):
    nz, rows, front = m0_ref.shape
    zi, ncpl = nz * rows, u_ref.shape[-1]
    m0 = m0_ref[...].reshape(zi, front)
    m1 = m1_ref[...].reshape(zi, front)
    y = -(mm(h_ref[:, :zi], m0) + mm(h_ref[:, zi:], m1))
    y = y.astype(BF)
    y_ref[...] = y
    mine, other = by_core(core[0], y[:, : front // 2], y[:, front // 2 :])
    u = jnp.zeros(u_ref.shape[1:], F32)
    for half, ref in ((mine, c0_ref), (other, c1_ref)):
        for i in range(front // ncpl):
            block = ref[:, :, i * ncpl : (i + 1) * ncpl].reshape(zi, ncpl)
            u += mm(half[:, i * zi : (i + 1) * zi], block)
    u_ref[...] = jnp.broadcast_to(u.astype(BF)[None], u_ref.shape)


def select_kernel(at_ref, w_ref, out_ref):
    nz, rows, front = w_ref.shape
    zi, tile = nz * rows, out_ref.shape[0]
    ncol = out_ref.shape[1]
    at = at_ref[...]
    lane = lax.broadcasted_iota(jnp.int32, (tile, zi), 1)
    acc = jnp.zeros(out_ref.shape, F32)
    for i in range(front // ncol):
        hot = jnp.where(at - i * zi == lane, 1.0, 0.0).astype(BF)
        acc += mm(hot, w_ref[:, :, i * ncol : (i + 1) * ncol].reshape(zi, ncol))
    out_ref[...] = acc.astype(BF)


def root_kernel(nx, u_ref, r0_ref, r1_ref, pre_ref, y_ref, cpl_ref):
    n = u_ref.shape[-1]
    acc = pre_ref[...]
    sel = []
    for x in range(nx):
        u = sum(u_ref[j].astype(F32) for j in range(x, u_ref.shape[0], nx))
        sel.append(r0_ref[x * n : (x + 1) * n, :] + r1_ref[x * n : (x + 1) * n, :])
        acc -= mm(u.astype(BF), sel[x])
    y = acc.astype(BF)
    y_ref[...] = y
    for x in range(nx):
        cpl_ref[x] = mm_t(y, sel[x]).astype(BF)


def back_kernel(core, cp_ref, y0, y1, y2, y3, m0_ref, m1_ref, c0_ref, c1_ref, out_ref):
    nz, rows, front = m0_ref.shape
    zi, ncpl = nz * rows, cp_ref.shape[-1]
    cp = sum(cp_ref[j].astype(F32) for j in range(cp_ref.shape[0])).astype(BF)
    halves = []
    for ref in (c0_ref, c1_ref):
        parts = [
            mm_t(cp, ref[:, :, i * ncpl : (i + 1) * ncpl].reshape(zi, ncpl))
            for i in range(front // ncpl)
        ]
        halves.append(jnp.concatenate(parts, 1))
    full = jnp.concatenate(by_core(core[0], halves[0], halves[1]), 1)
    y = sum(r[...].astype(F32) for r in (y0, y1, y2, y3))
    w = (y - full).astype(BF)
    x0 = mm_t(w, m0_ref[...].reshape(zi, front))
    x1 = mm_t(w, m1_ref[...].reshape(zi, front))
    x = jnp.concatenate([x0, x1], 1).astype(BF)
    out_ref[...] = jnp.broadcast_to(x[None], out_ref.shape)


def leaf_kernel(parent, size, first, core, x0_ref, x1_ref, cw_ref, y_ref, out_ref):
    leaf = pl.program_id(0)
    half = x0_ref.shape[2] // 2
    x0 = x0_ref[0]
    x1 = jnp.concatenate([x1_ref[0, :, half:], x1_ref[0, :, :half]], 1)
    x = jnp.concatenate(by_core(core[0], x0, x1), 0)
    w = y_ref[0] - mm(x, cw_ref[0])
    lane = first[0] + lax.broadcasted_iota(jnp.int32, w.shape, 1)
    w = jnp.where(lane < size[leaf], w, 0.0).astype(BF)
    out_ref[...] = jnp.broadcast_to(w[None, None], out_ref.shape)


def body(
    leaf_grad,
    leaf_inv,
    leaf_cpl,
    leaf_size,
    leaf_parent,
    leaf_map,
    mid_grad,
    mid_inv,
    mid_cpl,
    mid_map,
    root_grad,
    root_inv,
):
    ny, nz, nc, nx = (lax.axis_size(a) for a in ("y", "z", "c", "x"))
    iy, iz, ic, ix = (lax.axis_index(a) for a in ("y", "z", "c", "x"))
    nl, share, order = leaf_inv.shape
    nk = leaf_grad.shape[1]
    hk = nk // nc
    rows, front = mid_inv.shape[1:]
    ncpl = leaf_cpl.shape[2]
    nmid = mid_map.shape[0]
    zi = nz * rows
    half = front // nc
    width = front // ny
    blk = front // nx
    core = ic.astype(jnp.int32).reshape(1)

    def pick(first, second):
        return jnp.where(ic == 0, first, second)

    def place(m, y0):
        c = (m // rows % nc) ^ ic
        z = m // (rows * nc) % nz
        y = (m // (rows * nc * nz) - y0) % ny
        return (c * ny + y) * zi + z * rows + m % rows

    def half_sum(v, turn=lambda t: t):
        lo, hi = v[..., :hk, :], v[..., hk:, :]
        return pick(lo, hi) + swap(turn(pick(hi, lo).astype(BF))).astype(F32)

    own = iy * zi + iz * rows

    with jax.named_scope("leaf_forward"):
        live = (ix * share + lax.iota(jnp.int32, share))[None, :] < leaf_size[:, None]
        live = live[:, None, :]
        inv4 = leaf_inv.reshape(nl, share, nx, share)
        part = jnp.einsum(
            "lkp,lpxq->xlkq", leaf_grad, inv4, preferred_element_type=F32
        ).astype(BF)
        leaf_y = jnp.where(live, jnp.sum(a2a(part, "x").astype(F32), 0), 0.0)
        leaf_yb = leaf_y.astype(BF)

    with jax.named_scope("gather"):
        place_x = ix.astype(jnp.int32).reshape(1)
        mine, rinv_x = pl.pallas_call(
            root_pack_kernel,
            grid_spec=pltpu.PrefetchScalarGridSpec(
                num_scalar_prefetch=1,
                grid=(1,),
                in_specs=[
                    pl.BlockSpec((rows, blk), lambda i, at: (0, at[0])),
                    pl.BlockSpec((nk, rows), lambda i, at: (0, 0)),
                    pl.BlockSpec((rows, ncpl), lambda i, at: (0, 0)),
                ],
                out_specs=[
                    pl.BlockSpec((2 * rows + nk, blk), lambda i, at: (0, 0)),
                    pl.BlockSpec((rows, blk), lambda i, at: (0, 0)),
                ],
            ),
            out_shape=[
                jax.ShapeDtypeStruct((2 * rows + nk, blk), BF),
                jax.ShapeDtypeStruct((rows, blk), BF),
            ],
            compiler_params=PARAMS,
            name="root_pack",
        )(place_x, root_inv, root_grad, mid_cpl[0])
        got = ahead(mine, "y")
        g = front // blk
        payload = pl.pallas_call(
            functools.partial(pack_kernel, nk),
            in_specs=[SM] + [VM] * 5,
            out_specs=VM,
            out_shape=jax.ShapeDtypeStruct((3 * rows + nk // g, front), BF),
            compiler_params=PARAMS,
            name="pack",
        )(iy.astype(jnp.int32).reshape(1), after(mid_inv[0], part), *got)
        wide = lax.all_gather(payload, "z", axis=0)

    with jax.named_scope("leaf_spread"):
        target = place(leaf_map, 0)
        hot = (target[:, :, None] == lax.iota(jnp.int32, front)).astype(BF)
        cpl_wide = jnp.einsum(
            "lcn,lpc->lnp", hot, leaf_cpl, preferred_element_type=F32
        ).astype(BF)
        parent_of = jnp.arange(nmid)[:, None] == leaf_parent[None, :]
        lhs = jnp.where(parent_of[:, None, :, None], leaf_yb.transpose(1, 0, 2)[None], 0)
        placed = jnp.einsum(
            "mlp,lnp->mn",
            lhs.reshape(nmid * nk, nl, share),
            cpl_wide,
            preferred_element_type=F32,
        ).reshape(nmid, nk, front)
        here = own + lax.iota(jnp.int32, rows)
        hot_here = (here[:, None] == lax.iota(jnp.int32, front)[None, :]).astype(BF)
        grad = mm(mid_grad[:, 0, :], hot_here)
        placed = placed - jnp.where(jnp.arange(nmid)[:, None, None] == ix, grad[None], 0.0)

    with jax.named_scope("contrib_sum"):
        s = half_sum(placed, flip).astype(BF)
        s = s.reshape(nx, hk, nc, ny, zi).transpose(3, 0, 1, 2, 4).reshape(ny * nx, hk, width)
        s_own = jnp.sum(a2a(s, ("y", "x")).astype(F32), 0).astype(BF)
        s = jnp.sum(spread(s_own, "z").astype(F32), 0)
        contrib = s.astype(BF)

    with jax.named_scope("gather"):
        w0 = after(wide, contrib)
        w1 = swap(w0)
        pre = jnp.sum(w0[:, 3 * rows :].astype(F32), 0)
        pre = half_sum(jnp.concatenate(jnp.split(pre, g, 1), 0))

        def part_of(i):
            return pl.BlockSpec((nz, rows, front), lambda *_: (0, i, 0))

        at = place(mid_map, iy).reshape(-1, 1)
        tile = 256

        rsel0 = pl.pallas_call(
            select_kernel,
            grid=(nmid * ncpl // tile,),
            in_specs=[pl.BlockSpec((tile, 1), lambda i: (i, 0)), part_of(2)],
            out_specs=pl.BlockSpec((tile, blk), lambda i: (i, 0)),
            out_shape=jax.ShapeDtypeStruct((nmid * ncpl, blk), BF),
            compiler_params=PARAMS,
            name="root_select",
        )(at, w0)
        contrib = after(contrib, rsel0)
        rsel1 = swap(rsel0)

    def whole(shape):
        return pl.BlockSpec(shape, lambda *_: (0,) * len(shape))

    with jax.named_scope("mid_forward"):
        part_y, u = pl.pallas_call(
            mid_kernel,
            grid=(1,),
            in_specs=[SM, whole((hk, width)), part_of(0), part_of(0), part_of(1), part_of(1)],
            out_specs=[whole((hk, front)), whole((ny * nx, hk, ncpl))],
            out_shape=[
                jax.ShapeDtypeStruct((hk, front), BF),
                jax.ShapeDtypeStruct((ny * nx, hk, ncpl), BF),
            ],
            compiler_params=PARAMS,
            name="mid_forward",
        )(core, contrib, w0, w1, w0, w1)
        u = a2a(u, ("y", "x"))

    with jax.named_scope("root"):
        root_y, coupled = pl.pallas_call(
            functools.partial(root_kernel, nx),
            in_specs=[VM] * 4,
            out_specs=[VM] * 2,
            out_shape=[
                jax.ShapeDtypeStruct((hk, blk), BF),
                jax.ShapeDtypeStruct((nx, hk, ncpl), BF),
            ],
            compiler_params=PARAMS,
            name="root",
        )(u, rsel0, rsel1, pre)
        ys = ahead(after(part_y, root_y), "y")
        coupled = a2a(coupled, "x")

    with jax.named_scope("mid_backward"):
        mx = pl.pallas_call(
            back_kernel,
            grid=(1,),
            in_specs=[SM, whole((nx, hk, ncpl))]
            + [whole((hk, front))] * ny
            + [part_of(0), part_of(0), part_of(1), part_of(1)],
            out_specs=whole((ny * nx, hk, width)),
            out_shape=jax.ShapeDtypeStruct((ny * nx, hk, width), BF),
            compiler_params=PARAMS,
            name="mid_backward",
        )(core, coupled, *ys, w0, w1, w0, w1)
        both = jnp.concatenate([rinv_x, swap(rinv_x)], 0)
        rx = sum(ahead(mm_t(root_y, both), "x"))
        mx = after(a2a(mx, ("y", "x")), rx).reshape(ny, nx, hk, nc, zi)
        mx = mx.transpose(1, 2, 3, 0, 4).reshape(nx, hk, front)
        mo = swap(mx)

    with jax.named_scope("leaf_backward"):
        w = pl.pallas_call(
            leaf_kernel,
            grid_spec=pltpu.PrefetchScalarGridSpec(
                num_scalar_prefetch=4,
                grid=(nl,),
                in_specs=[
                    pl.BlockSpec((1, hk, front), lambda i, parent, *_: (parent[i], 0, 0)),
                    pl.BlockSpec((1, hk, front), lambda i, parent, *_: (parent[i], 0, 0)),
                    pl.BlockSpec((1, front, share), lambda i, *_: (i, 0, 0)),
                    pl.BlockSpec((1, nk, share), lambda i, *_: (i, 0, 0)),
                ],
                out_specs=pl.BlockSpec((nx, 1, nk, share), lambda i, *_: (0, i, 0, 0)),
            ),
            out_shape=jax.ShapeDtypeStruct((nx, nl, nk, share), BF),
            compiler_params=PARAMS,
            name="leaf_backward",
        )(leaf_parent, leaf_size, (ix * share).astype(jnp.int32).reshape(1), core, mx, mo, cpl_wide, leaf_y)

    with jax.named_scope("outputs"):

        def mine_of(v, at):
            v = lax.dynamic_index_in_dim(v, ix, 0, keepdims=False)
            return lax.dynamic_slice(v, (0, at), (hk, rows))

        om = mine_of(mx, own), mine_of(mo, half + own)
        out_m = jnp.concatenate([pick(*om), pick(om[1], om[0])], 0)
        rx = after(rx, w)
        ro = swap(rx[:, rows:])
        out_r = jnp.concatenate(
            [pick(rx[:, :rows], ro), pick(ro, rx[:, :rows])], 0
        )

    with jax.named_scope("leaf_result"):
        w = a2a(w, "x")
        w, out_r = lax.optimization_barrier((w, out_r))
        leaf_x = jnp.einsum("xlkq,lpxq->lkp", w, inv4, preferred_element_type=F32)
    return leaf_x, out_m.astype(F32)[:, None, :], out_r


def solution(mesh):
    grid = Mesh(mesh.devices.reshape(4, 8, 2, 4), ("y", "z", "c", "x"))
    row = ("y", "z", "c")
    placed = (
        P(row, None, "x"),
        P(row, "x", None),
        P(row, "x", None),
        P(row),
        P(row),
        P(row, None),
        P(None, "x", row),
        P("x", row, None),
        P("x", row, None),
        P(),
        P(None, row),
        P(row, None),
    )
    return jax.shard_map(
        body,
        mesh=grid,
        in_specs=placed,
        out_specs=(P(row, None, "x"), P(None, "x", row), P(None, row)),
        check_vma=False,
    )
```

```python
import functools

import jax
import jax.numpy as jnp
from jax import lax
from jax.experimental import pallas as pl
from jax.experimental.pallas import tpu as pltpu
from jax.sharding import Mesh, PartitionSpec as P

BF = jnp.bfloat16
F32 = jnp.float32
VM = pl.BlockSpec(memory_space=pltpu.VMEM)
SM = pl.BlockSpec(memory_space=pltpu.SMEM)
PARAMS = pltpu.CompilerParams(vmem_limit_bytes=60 * 2**20)


def mm(a, b):
    return jnp.dot(a, b, preferred_element_type=F32)


def mm_t(a, b):
    return lax.dot_general(a, b, (((1,), (1,)), ((), ())), preferred_element_type=F32)


def a2a(v, axes):
    return lax.all_to_all(v, axes, 0, 0, tiled=True)


def spread(v, axes):
    n = lax.axis_size(axes)
    return a2a(jnp.broadcast_to(v[None], (n,) + v.shape), axes)


def swap(v):
    return lax.ppermute(v, "c", [(0, 1), (1, 0)])


def ahead(v, axis):
    n = lax.axis_size(axis)
    return [v] + [
        lax.ppermute(v, axis, [((i + k) % n, i) for i in range(n)]) for k in range(1, n)
    ]


def flip(v):
    n = v.shape[-1] // 2
    return jnp.concatenate([v[..., n:], v[..., :n]], -1)


def after(v, *first):
    return lax.optimization_barrier((v,) + first)[0]


def by_core(core, first, second):
    return jnp.where(core == 0, first, second), jnp.where(core == 0, second, first)


def root_pack_kernel(at, inv_ref, grad_ref, cpl_ref, out_ref, keep_ref):
    rows, nk = inv_ref.shape[0], grad_ref.shape[0]
    keep_ref[...] = inv_ref[...]
    out_ref[:rows, :] = inv_ref[...]
    out_ref[rows : rows + nk, :] = mm(grad_ref[...], inv_ref[...]).astype(BF)
    out_ref[rows + nk :, :] = cpl_ref[...]


def pack_kernel(nk, iy, inv_ref, g0, g1, g2, g3, out_ref):
    rows, front = inv_ref.shape
    got = (g0, g1, g2, g3)
    n = g0.shape[1]
    lane = lax.broadcasted_iota(jnp.int32, (rows, 128), 1) // 32
    for pair in range(front // 256):
        a = inv_ref[:, pair * 256 : pair * 256 + 128].astype(F32)
        b = inv_ref[:, pair * 256 + 128 : pair * 256 + 256].astype(F32)
        for c in range(2):
            if c == 0:
                parts = [a, pltpu.roll(a, 96, 1), pltpu.roll(b, 64, 1), pltpu.roll(b, 32, 1)]
            else:
                parts = [pltpu.roll(a, 96, 1), pltpu.roll(a, 64, 1), pltpu.roll(b, 32, 1), b]
            v = jnp.where(
                lane == 0,
                parts[0],
                jnp.where(lane == 1, parts[1], jnp.where(lane == 2, parts[2], parts[3])),
            )
            at = c * (front // 2) + pair * 128
            out_ref[:rows, at : at + 128] = v.astype(BF)
    for i, ref in enumerate(got):
        out_ref[2 * rows : 3 * rows, i * n : (i + 1) * n] = ref[:rows, :]
        s = lax.rem(iy[0] + i, len(got))
        for j in range(len(got)):

            @pl.when(s == j)
            def _():
                out_ref[rows : 2 * rows, j * n : (j + 1) * n] = ref[rows + nk :, :]

    pre = sum(ref[rows : rows + nk, :].astype(F32) for ref in got).astype(BF)
    step = nk // len(got)
    for i in range(len(got)):
        out_ref[3 * rows :, i * n : (i + 1) * n] = pre[i * step : (i + 1) * step, :]


def mid_kernel(core, h_ref, m0_ref, m1_ref, c0_ref, c1_ref, y_ref, u_ref):
    nz, rows, front = m0_ref.shape
    zi, ncpl = nz * rows, u_ref.shape[-1]
    m0 = m0_ref[...].reshape(zi, front)
    m1 = m1_ref[...].reshape(zi, front)
    y = -(mm(h_ref[:, :zi], m0) + mm(h_ref[:, zi:], m1))
    y = y.astype(BF)
    y_ref[...] = y
    mine, other = by_core(core[0], y[:, : front // 2], y[:, front // 2 :])
    u = jnp.zeros(u_ref.shape[1:], F32)
    for half, ref in ((mine, c0_ref), (other, c1_ref)):
        for i in range(front // ncpl):
            block = ref[:, :, i * ncpl : (i + 1) * ncpl].reshape(zi, ncpl)
            u += mm(half[:, i * zi : (i + 1) * zi], block)
    u_ref[...] = jnp.broadcast_to(u.astype(BF)[None], u_ref.shape)


def select_kernel(at_ref, w_ref, out_ref):
    nz, rows, front = w_ref.shape
    zi, tile = nz * rows, out_ref.shape[0]
    ncol = out_ref.shape[1]
    at = jnp.broadcast_to(at_ref[0], (zi, tile)).T
    lane = lax.broadcasted_iota(jnp.int32, (tile, zi), 1)
    acc = jnp.zeros(out_ref.shape, F32)
    for i in range(front // ncol):
        hot = jnp.where(at - i * zi == lane, 1.0, 0.0).astype(BF)
        acc += mm(hot, w_ref[:, :, i * ncol : (i + 1) * ncol].reshape(zi, ncol))
    out_ref[...] = acc.astype(BF)


def root_kernel(nx, u_ref, r0_ref, r1_ref, pre_ref, w0_ref, w1_ref, ly_ref, y_ref, cpl_ref):
    n = u_ref.shape[-1]
    acc = pre_ref[...]
    sel = []
    for x in range(nx):
        u = sum(u_ref[j].astype(F32) for j in range(x, u_ref.shape[0], nx))
        sel.append(r0_ref[x * n : (x + 1) * n, :] + r1_ref[x * n : (x + 1) * n, :])
        acc -= mm(u.astype(BF), sel[x])
    y = acc.astype(BF)
    y_ref[...] = y
    both = jnp.concatenate([w0_ref[...], w1_ref[...]], 0)
    both = jnp.concatenate([both, jnp.zeros((128 - both.shape[0], both.shape[1]), BF)], 0)
    part = mm_t(y, both).astype(BF)
    hk = y.shape[0]
    share = ly_ref.shape[2]
    for x in range(nx):
        cpl_ref[x, :hk, :n] = mm_t(y, sel[x]).astype(BF)
        cpl_ref[x, :hk, n:] = part
        for i in range(ly_ref.shape[0]):
            for h in range(2):
                cpl_ref[x, (i + 1) * hk : (i + 2) * hk, h * share : (h + 1) * share] = ly_ref[
                    i, h * hk : (h + 1) * hk, :
                ]


def back_kernel(core, cp_ref, y0, y1, y2, y3, m0_ref, m1_ref, c0_ref, c1_ref, out_ref):
    nz, rows, front = m0_ref.shape
    zi, ncpl = nz * rows, cp_ref.shape[-1] - 128
    cp = sum(cp_ref[j, :, :ncpl].astype(F32) for j in range(cp_ref.shape[0])).astype(BF)
    halves = []
    for ref in (c0_ref, c1_ref):
        parts = [
            mm_t(cp, ref[:, :, i * ncpl : (i + 1) * ncpl].reshape(zi, ncpl))
            for i in range(front // ncpl)
        ]
        halves.append(jnp.concatenate(parts, 1))
    full = jnp.concatenate(by_core(core[0], halves[0], halves[1]), 1)
    y = sum(r[...].astype(F32) for r in (y0, y1, y2, y3))
    w = (y - full).astype(BF)
    x0 = mm_t(w, m0_ref[...].reshape(zi, front))
    x1 = mm_t(w, m1_ref[...].reshape(zi, front))
    x = jnp.concatenate([x0, x1], 1).astype(BF)
    out_ref[...] = jnp.broadcast_to(x[None], out_ref.shape)


def leaf_kernel(parent, core, x0_ref, x1_ref, at_ref, n_ref, base_ref, out_ref):
    half = x0_ref.shape[2] // 2
    ncpl, chunk = at_ref.shape[2], 256
    x1 = jnp.concatenate([x1_ref[0, :, half:], x1_ref[0, :, :half]], 1)
    x = jnp.concatenate(by_core(core[0], x0_ref[0], x1), 0)
    at = at_ref[0]
    place = lax.broadcasted_iota(jnp.int32, (chunk, ncpl), 0)
    acc = jnp.zeros((x.shape[0], ncpl), F32)
    for i in range(x.shape[1] // chunk):
        hot = jnp.where(at - i * chunk == place, 1.0, 0.0).astype(BF)
        acc += mm(x[:, i * chunk : (i + 1) * chunk], hot)
    out_ref[0] = base_ref[0] - mm_t(acc.astype(BF), n_ref[0])


def body(
    leaf_grad,
    leaf_inv,
    leaf_cpl,
    leaf_size,
    leaf_parent,
    leaf_map,
    mid_grad,
    mid_inv,
    mid_cpl,
    mid_map,
    root_grad,
    root_inv,
):
    ny, nz, nc, nx = (lax.axis_size(a) for a in ("y", "z", "c", "x"))
    iy, iz, ic, ix = (lax.axis_index(a) for a in ("y", "z", "c", "x"))
    nl, share, order = leaf_inv.shape
    nk = leaf_grad.shape[1]
    hk = nk // nc
    rows, front = mid_inv.shape[1:]
    ncpl = leaf_cpl.shape[2]
    nmid = mid_map.shape[0]
    zi = nz * rows
    half = front // nc
    width = front // ny
    blk = front // nx
    core = ic.astype(jnp.int32).reshape(1)

    def pick(first, second):
        return jnp.where(ic == 0, first, second)

    def place(m, y0):
        c = (m // rows % nc) ^ ic
        z = m // (rows * nc) % nz
        y = (m // (rows * nc * nz) - y0) % ny
        return (c * ny + y) * zi + z * rows + m % rows

    def half_sum(v, turn=lambda t: t):
        lo, hi = v[..., :hk, :], v[..., hk:, :]
        return pick(lo, hi) + swap(turn(pick(hi, lo).astype(BF))).astype(F32)

    own = iy * zi + iz * rows

    with jax.named_scope("leaf_forward"):
        live = (ix * share + lax.iota(jnp.int32, share))[None, :] < leaf_size[:, None]
        live = live[:, None, :]
        inv4 = leaf_inv.reshape(nl, share, nx, share)
        part = jnp.einsum(
            "lkp,lpxq->xlkq", leaf_grad, inv4, preferred_element_type=F32
        ).astype(BF)
        leaf_y = jnp.where(live, jnp.sum(a2a(part, "x").astype(F32), 0), 0.0)
        leaf_yb = leaf_y.astype(BF)

    with jax.named_scope("gather"):
        place_x = ix.astype(jnp.int32).reshape(1)
        mine, rinv_x = pl.pallas_call(
            root_pack_kernel,
            grid_spec=pltpu.PrefetchScalarGridSpec(
                num_scalar_prefetch=1,
                grid=(1,),
                in_specs=[
                    pl.BlockSpec((rows, blk), lambda i, at: (0, at[0])),
                    pl.BlockSpec((nk, rows), lambda i, at: (0, 0)),
                    pl.BlockSpec((rows, ncpl), lambda i, at: (0, 0)),
                ],
                out_specs=[
                    pl.BlockSpec((2 * rows + nk, blk), lambda i, at: (0, 0)),
                    pl.BlockSpec((rows, blk), lambda i, at: (0, 0)),
                ],
            ),
            out_shape=[
                jax.ShapeDtypeStruct((2 * rows + nk, blk), BF),
                jax.ShapeDtypeStruct((rows, blk), BF),
            ],
            compiler_params=PARAMS,
            name="root_pack",
        )(place_x, root_inv, root_grad, mid_cpl[0])
        rinv_o = swap(rinv_x)
        got = ahead(mine, "y")
        g = front // blk
        payload = pl.pallas_call(
            functools.partial(pack_kernel, nk),
            in_specs=[SM] + [VM] * 5,
            out_specs=VM,
            out_shape=jax.ShapeDtypeStruct((3 * rows + nk // g, front), BF),
            compiler_params=PARAMS,
            name="pack",
        )(iy.astype(jnp.int32).reshape(1), after(mid_inv[0], part), *got)
        wide = lax.all_gather(payload, "z", axis=0)

    with jax.named_scope("leaf_spread"):
        target = place(leaf_map, 0)
        hot = (target[:, :, None] == lax.iota(jnp.int32, front)).astype(BF)
        cpl_wide = jnp.einsum(
            "lcn,lpc->lnp", hot, leaf_cpl, preferred_element_type=F32
        ).astype(BF)
        parent_of = jnp.arange(nmid)[:, None] == leaf_parent[None, :]
        lhs = jnp.where(parent_of[:, None, :, None], leaf_yb.transpose(1, 0, 2)[None], 0)
        placed = jnp.einsum(
            "mlp,lnp->mn",
            lhs.reshape(nmid * nk, nl, share),
            cpl_wide,
            preferred_element_type=F32,
        ).reshape(nmid, nk, front)
        here = own + lax.iota(jnp.int32, rows)
        hot_here = (here[:, None] == lax.iota(jnp.int32, front)[None, :]).astype(BF)
        grad = mm(mid_grad[:, 0, :], hot_here)
        placed = placed - jnp.where(jnp.arange(nmid)[:, None, None] == ix, grad[None], 0.0)

    with jax.named_scope("contrib_sum"):
        s = half_sum(placed, flip).astype(BF)
        s = s.reshape(nx, hk, nc, ny, zi).transpose(3, 0, 1, 2, 4).reshape(ny * nx, hk, width)
        s_own = jnp.sum(a2a(s, ("y", "x")).astype(F32), 0).astype(BF)
        s = jnp.sum(spread(s_own, "z").astype(F32), 0)
        contrib = s.astype(BF)
        cpl_all = lax.all_gather(after(leaf_cpl, s_own), "x", axis=0)

    with jax.named_scope("gather"):
        w0 = after(wide, contrib)
        w1 = swap(w0)
        def part_of(i):
            return pl.BlockSpec((nz, rows, front), lambda *_: (0, i, 0))

        tile = 256
        at = place(mid_map, iy).reshape(-1, 1, tile)

        rsel0 = pl.pallas_call(
            select_kernel,
            grid=(nmid * ncpl // tile,),
            in_specs=[pl.BlockSpec((1, 1, tile), lambda i: (i, 0, 0)), part_of(2)],
            out_specs=pl.BlockSpec((tile, blk), lambda i: (i, 0)),
            out_shape=jax.ShapeDtypeStruct((nmid * ncpl, blk), BF),
            compiler_params=PARAMS,
            name="root_select",
        )(at, w0)
        contrib = after(contrib, rsel0)
        rsel1 = swap(rsel0)

    def whole(shape):
        return pl.BlockSpec(shape, lambda *_: (0,) * len(shape))

    with jax.named_scope("mid_forward"):
        part_y, u = pl.pallas_call(
            mid_kernel,
            grid=(1,),
            in_specs=[SM, whole((hk, width)), part_of(0), part_of(0), part_of(1), part_of(1)],
            out_specs=[whole((hk, front)), whole((ny * nx, hk, ncpl))],
            out_shape=[
                jax.ShapeDtypeStruct((hk, front), BF),
                jax.ShapeDtypeStruct((ny * nx, hk, ncpl), BF),
            ],
            compiler_params=PARAMS,
            name="mid_forward",
        )(core, contrib, w0, w1, w0, w1)
        pre = jnp.sum(after(w0, part_y)[:, 3 * rows :].astype(F32), 0)
        pre = half_sum(jnp.concatenate(jnp.split(pre, g, 1), 0))
        u = a2a(u, ("y", "x"))

    with jax.named_scope("root"):
        root_y, coupled = pl.pallas_call(
            functools.partial(root_kernel, nx),
            in_specs=[VM] * 7,
            out_specs=[VM] * 2,
            out_shape=[
                jax.ShapeDtypeStruct((hk, blk), BF),
                jax.ShapeDtypeStruct((nx, hk * (1 + nl), ncpl + 128), BF),
            ],
            compiler_params=PARAMS,
            name="root",
        )(u, rsel0, rsel1, pre, rinv_x, rinv_o, leaf_yb)
        ys = ahead(after(part_y, root_y), "y")
        coupled = a2a(coupled, "x")

    with jax.named_scope("mid_backward"):
        mx = pl.pallas_call(
            back_kernel,
            grid=(1,),
            in_specs=[SM, whole((nx, hk, ncpl + 128))]
            + [whole((hk, front))] * ny
            + [part_of(0), part_of(0), part_of(1), part_of(1)],
            out_specs=whole((ny * nx, hk, width)),
            out_shape=jax.ShapeDtypeStruct((ny * nx, hk, width), BF),
            compiler_params=PARAMS,
            name="mid_backward",
        )(core, coupled, *ys, w0, w1, w0, w1)
        rx = jnp.sum(coupled[:, :hk, ncpl : ncpl + nc * rows].astype(F32), 0)
        alive = lax.iota(jnp.int32, order)[None, :] < leaf_size[:, None]
        inv_m = jnp.where(alive[:, None, :], after(leaf_inv, root_y), 0)
        nmat = jnp.einsum(
            "lpxq,xlqc->lpc",
            inv_m.reshape(nl, share, nx, share),
            after(cpl_all, mx),
            preferred_element_type=F32,
        ).astype(BF)
        y_all = coupled[:, hk:, :ncpl].reshape(nx, nl, hk, 2, share)
        y_all = y_all.transpose(0, 1, 3, 2, 4).reshape(nx, nl, nk, share)
        base = jnp.einsum("xlkq,lpxq->lkp", y_all, inv4, preferred_element_type=F32)
        mx = after(a2a(mx, ("y", "x")), nmat, base).reshape(ny, nx, hk, nc, zi)
        mx = mx.transpose(1, 2, 3, 0, 4).reshape(nx, hk, front)
        mo = swap(mx)

    with jax.named_scope("leaf_backward"):
        leaf_x = pl.pallas_call(
            leaf_kernel,
            grid_spec=pltpu.PrefetchScalarGridSpec(
                num_scalar_prefetch=2,
                grid=(nl,),
                in_specs=[
                    pl.BlockSpec((1, hk, front), lambda i, parent, *_: (parent[i], 0, 0)),
                    pl.BlockSpec((1, hk, front), lambda i, parent, *_: (parent[i], 0, 0)),
                    pl.BlockSpec((1, 1, ncpl), lambda i, *_: (i, 0, 0)),
                    pl.BlockSpec((1, share, ncpl), lambda i, *_: (i, 0, 0)),
                    pl.BlockSpec((1, nk, share), lambda i, *_: (i, 0, 0)),
                ],
                out_specs=pl.BlockSpec((1, nk, share), lambda i, *_: (i, 0, 0)),
            ),
            out_shape=jax.ShapeDtypeStruct((nl, nk, share), F32),
            compiler_params=PARAMS,
            name="leaf_backward",
        )(leaf_parent, core, mx, mo, target[:, None, :], nmat, base)

    with jax.named_scope("outputs"):

        def mine_of(v, at):
            v = lax.dynamic_index_in_dim(v, ix, 0, keepdims=False)
            return lax.dynamic_slice(v, (0, at), (hk, rows))

        om = mine_of(mx, own), mine_of(mo, half + own)
        out_m = jnp.concatenate([pick(*om), pick(om[1], om[0])], 0)
        ro = swap(rx[:, rows:])
        out_r = jnp.concatenate(
            [pick(rx[:, :rows], ro), pick(ro, rx[:, :rows])], 0
        )
    return leaf_x, out_m.astype(F32)[:, None, :], out_r


def solution(mesh):
    grid = Mesh(mesh.devices.reshape(4, 8, 2, 4), ("y", "z", "c", "x"))
    row = ("y", "z", "c")
    placed = (
        P(row, None, "x"),
        P(row, "x", None),
        P(row, "x", None),
        P(row),
        P(row),
        P(row, None),
        P(None, "x", row),
        P("x", row, None),
        P("x", row, None),
        P(),
        P(None, row),
        P(row, None),
    )
    return jax.shard_map(
        body,
        mesh=grid,
        in_specs=placed,
        out_specs=(P(row, None, "x"), P(None, "x", row), P(None, row)),
        check_vma=False,
    )
```

```python
import functools

import jax
import jax.numpy as jnp
from jax import lax
from jax.experimental import pallas as pl
from jax.experimental.pallas import tpu as pltpu
from jax.sharding import Mesh, PartitionSpec as P

BF = jnp.bfloat16
F32 = jnp.float32
VM = pl.BlockSpec(memory_space=pltpu.VMEM)
SM = pl.BlockSpec(memory_space=pltpu.SMEM)
PARAMS = pltpu.CompilerParams(vmem_limit_bytes=60 * 2**20)


def mm(a, b):
    return jnp.dot(a, b, preferred_element_type=F32)


def mm_t(a, b):
    return lax.dot_general(a, b, (((1,), (1,)), ((), ())), preferred_element_type=F32)


def a2a(v, axes):
    return lax.all_to_all(v, axes, 0, 0, tiled=True)


def spread(v, axes):
    n = lax.axis_size(axes)
    return a2a(jnp.broadcast_to(v[None], (n,) + v.shape), axes)


def swap(v):
    return lax.ppermute(v, "c", [(0, 1), (1, 0)])


def ahead(v, axis):
    n = lax.axis_size(axis)
    return [v] + [
        lax.ppermute(v, axis, [((i + k) % n, i) for i in range(n)]) for k in range(1, n)
    ]


def flip(v):
    n = v.shape[-1] // 2
    return jnp.concatenate([v[..., n:], v[..., :n]], -1)


def after(v, *first):
    return lax.optimization_barrier((v,) + first)[0]


def by_core(core, first, second):
    return jnp.where(core == 0, first, second), jnp.where(core == 0, second, first)


def root_pack_kernel(at, inv_ref, grad_ref, cpl_ref, out_ref, keep_ref):
    rows, nk = inv_ref.shape[0], grad_ref.shape[0]
    keep_ref[...] = inv_ref[...]
    out_ref[:rows, :] = inv_ref[...]
    out_ref[rows : rows + nk, :] = mm(grad_ref[...], inv_ref[...]).astype(BF)
    out_ref[rows + nk :, :] = cpl_ref[...]


def pack_kernel(nk, iy, inv_ref, g0, g1, g2, g3, out_ref):
    rows, front = inv_ref.shape
    got = (g0, g1, g2, g3)
    n = g0.shape[1]
    lane = lax.broadcasted_iota(jnp.int32, (rows, 128), 1) // 32
    for pair in range(front // 256):
        a = inv_ref[:, pair * 256 : pair * 256 + 128].astype(F32)
        b = inv_ref[:, pair * 256 + 128 : pair * 256 + 256].astype(F32)
        for c in range(2):
            if c == 0:
                parts = [a, pltpu.roll(a, 96, 1), pltpu.roll(b, 64, 1), pltpu.roll(b, 32, 1)]
            else:
                parts = [pltpu.roll(a, 96, 1), pltpu.roll(a, 64, 1), pltpu.roll(b, 32, 1), b]
            v = jnp.where(
                lane == 0,
                parts[0],
                jnp.where(lane == 1, parts[1], jnp.where(lane == 2, parts[2], parts[3])),
            )
            at = c * (front // 2) + pair * 128
            out_ref[:rows, at : at + 128] = v.astype(BF)
    for i, ref in enumerate(got):
        out_ref[2 * rows : 3 * rows, i * n : (i + 1) * n] = ref[:rows, :]
        s = lax.rem(iy[0] + i, len(got))
        for j in range(len(got)):

            @pl.when(s == j)
            def _():
                out_ref[rows : 2 * rows, j * n : (j + 1) * n] = ref[rows + nk :, :]

    pre = sum(ref[rows : rows + nk, :].astype(F32) for ref in got).astype(BF)
    step = nk // len(got)
    for i in range(len(got)):
        out_ref[3 * rows :, i * n : (i + 1) * n] = pre[i * step : (i + 1) * step, :]


def mid_kernel(core, h_ref, m0_ref, m1_ref, c0_ref, c1_ref, y_ref, u_ref):
    nz, rows, front = m0_ref.shape
    zi, ncpl = nz * rows, u_ref.shape[-1]
    m0 = m0_ref[...].reshape(zi, front)
    m1 = m1_ref[...].reshape(zi, front)
    y = -(mm(h_ref[:, :zi], m0) + mm(h_ref[:, zi:], m1))
    y = y.astype(BF)
    y_ref[...] = y
    mine, other = by_core(core[0], y[:, : front // 2], y[:, front // 2 :])
    u = jnp.zeros(u_ref.shape[1:], F32)
    for half, ref in ((mine, c0_ref), (other, c1_ref)):
        for i in range(front // ncpl):
            block = ref[:, :, i * ncpl : (i + 1) * ncpl].reshape(zi, ncpl)
            u += mm(half[:, i * zi : (i + 1) * zi], block)
    u_ref[...] = jnp.broadcast_to(u.astype(BF)[None], u_ref.shape)


def select_kernel(at_ref, w_ref, out_ref):
    nz, rows, front = w_ref.shape
    zi, tile = nz * rows, out_ref.shape[0]
    ncol = out_ref.shape[1]
    at = jnp.broadcast_to(at_ref[0], (zi, tile)).T
    lane = lax.broadcasted_iota(jnp.int32, (tile, zi), 1)
    acc = jnp.zeros(out_ref.shape, F32)
    for i in range(front // ncol):
        hot = jnp.where(at - i * zi == lane, 1.0, 0.0).astype(BF)
        acc += mm(hot, w_ref[:, :, i * ncol : (i + 1) * ncol].reshape(zi, ncol))
    out_ref[...] = acc.astype(BF)


def root_kernel(nx, u_ref, r0_ref, r1_ref, pre_ref, w0_ref, w1_ref, y_ref, cpl_ref):
    n = u_ref.shape[-1]
    acc = pre_ref[...]
    sel = []
    for x in range(nx):
        u = sum(u_ref[j].astype(F32) for j in range(x, u_ref.shape[0], nx))
        sel.append(r0_ref[x * n : (x + 1) * n, :] + r1_ref[x * n : (x + 1) * n, :])
        acc -= mm(u.astype(BF), sel[x])
    y = acc.astype(BF)
    y_ref[...] = y
    both = jnp.concatenate([w0_ref[...], w1_ref[...]], 0)
    both = jnp.concatenate([both, jnp.zeros((128 - both.shape[0], both.shape[1]), BF)], 0)
    part = mm_t(y, both).astype(BF)
    for x in range(nx):
        cpl_ref[x, :, :n] = mm_t(y, sel[x]).astype(BF)
        cpl_ref[x, :, n:] = part


def back_kernel(core, cp_ref, y0, y1, y2, y3, m0_ref, m1_ref, c0_ref, c1_ref, out_ref):
    nz, rows, front = m0_ref.shape
    zi, ncpl = nz * rows, cp_ref.shape[-1] - 128
    cp = sum(cp_ref[j, :, :ncpl].astype(F32) for j in range(cp_ref.shape[0])).astype(BF)
    halves = []
    for ref in (c0_ref, c1_ref):
        parts = [
            mm_t(cp, ref[:, :, i * ncpl : (i + 1) * ncpl].reshape(zi, ncpl))
            for i in range(front // ncpl)
        ]
        halves.append(jnp.concatenate(parts, 1))
    full = jnp.concatenate(by_core(core[0], halves[0], halves[1]), 1)
    y = sum(r[...].astype(F32) for r in (y0, y1, y2, y3))
    w = (y - full).astype(BF)
    x0 = mm_t(w, m0_ref[...].reshape(zi, front))
    x1 = mm_t(w, m1_ref[...].reshape(zi, front))
    x = jnp.concatenate([x0, x1], 1).astype(BF)
    out_ref[...] = jnp.broadcast_to(x[None], out_ref.shape)


def leaf_kernel(parent, core, x0_ref, x1_ref, at_ref, n_ref, base_ref, out_ref):
    half = x0_ref.shape[2] // 2
    ncpl, chunk = at_ref.shape[2], 256
    x1 = jnp.concatenate([x1_ref[0, :, half:], x1_ref[0, :, :half]], 1)
    x = jnp.concatenate(by_core(core[0], x0_ref[0], x1), 0)
    at = at_ref[0]
    place = lax.broadcasted_iota(jnp.int32, (chunk, ncpl), 0)
    acc = jnp.zeros((x.shape[0], ncpl), F32)
    for i in range(x.shape[1] // chunk):
        hot = jnp.where(at - i * chunk == place, 1.0, 0.0).astype(BF)
        acc += mm(x[:, i * chunk : (i + 1) * chunk], hot)
    out_ref[0] = base_ref[0] - mm_t(acc.astype(BF), n_ref[0])


def body(
    leaf_grad,
    leaf_inv,
    leaf_cpl,
    leaf_size,
    leaf_parent,
    leaf_map,
    mid_grad,
    mid_inv,
    mid_cpl,
    mid_map,
    root_grad,
    root_inv,
):
    ny, nz, nc, nx = (lax.axis_size(a) for a in ("y", "z", "c", "x"))
    iy, iz, ic, ix = (lax.axis_index(a) for a in ("y", "z", "c", "x"))
    nl, share, order = leaf_inv.shape
    nk = leaf_grad.shape[1]
    hk = nk // nc
    rows, front = mid_inv.shape[1:]
    ncpl = leaf_cpl.shape[2]
    nmid = mid_map.shape[0]
    zi = nz * rows
    half = front // nc
    width = front // ny
    blk = front // nx
    core = ic.astype(jnp.int32).reshape(1)

    def pick(first, second):
        return jnp.where(ic == 0, first, second)

    def place(m, y0):
        c = (m // rows % nc) ^ ic
        z = m // (rows * nc) % nz
        y = (m // (rows * nc * nz) - y0) % ny
        return (c * ny + y) * zi + z * rows + m % rows

    def half_sum(v, turn=lambda t: t):
        lo, hi = v[..., :hk, :], v[..., hk:, :]
        return pick(lo, hi) + swap(turn(pick(hi, lo).astype(BF))).astype(F32)

    own = iy * zi + iz * rows

    with jax.named_scope("leaf_forward"):
        live = (ix * share + lax.iota(jnp.int32, share))[None, :] < leaf_size[:, None]
        live = live[:, None, :]
        inv4 = leaf_inv.reshape(nl, share, nx, share)
        part = jnp.einsum(
            "lkp,lpxq->xlkq", leaf_grad, inv4, preferred_element_type=F32
        ).astype(BF)
        leaf_y = jnp.where(live, jnp.sum(a2a(part, "x").astype(F32), 0), 0.0)
        leaf_yb = leaf_y.astype(BF)

    with jax.named_scope("gather"):
        place_x = ix.astype(jnp.int32).reshape(1)
        mine, rinv_x = pl.pallas_call(
            root_pack_kernel,
            grid_spec=pltpu.PrefetchScalarGridSpec(
                num_scalar_prefetch=1,
                grid=(1,),
                in_specs=[
                    pl.BlockSpec((rows, blk), lambda i, at: (0, at[0])),
                    pl.BlockSpec((nk, rows), lambda i, at: (0, 0)),
                    pl.BlockSpec((rows, ncpl), lambda i, at: (0, 0)),
                ],
                out_specs=[
                    pl.BlockSpec((2 * rows + nk, blk), lambda i, at: (0, 0)),
                    pl.BlockSpec((rows, blk), lambda i, at: (0, 0)),
                ],
            ),
            out_shape=[
                jax.ShapeDtypeStruct((2 * rows + nk, blk), BF),
                jax.ShapeDtypeStruct((rows, blk), BF),
            ],
            compiler_params=PARAMS,
            name="root_pack",
        )(place_x, root_inv, root_grad, mid_cpl[0])
        rinv_o = swap(rinv_x)
        got = ahead(mine, "y")
        g = front // blk
        payload = pl.pallas_call(
            functools.partial(pack_kernel, nk),
            in_specs=[SM] + [VM] * 5,
            out_specs=VM,
            out_shape=jax.ShapeDtypeStruct((3 * rows + nk // g, front), BF),
            compiler_params=PARAMS,
            name="pack",
        )(iy.astype(jnp.int32).reshape(1), after(mid_inv[0], part), *got)
        wide = lax.all_gather(payload, "z", axis=0)

    with jax.named_scope("leaf_spread"):
        target = place(leaf_map, 0)
        hot = (target[:, :, None] == lax.iota(jnp.int32, front)).astype(BF)
        cpl_wide = jnp.einsum(
            "lcn,lpc->lnp", hot, leaf_cpl, preferred_element_type=F32
        ).astype(BF)
        parent_of = jnp.arange(nmid)[:, None] == leaf_parent[None, :]
        lhs = jnp.where(parent_of[:, None, :, None], leaf_yb.transpose(1, 0, 2)[None], 0)
        placed = jnp.einsum(
            "mlp,lnp->mn",
            lhs.reshape(nmid * nk, nl, share),
            cpl_wide,
            preferred_element_type=F32,
        ).reshape(nmid, nk, front)
        here = own + lax.iota(jnp.int32, rows)
        hot_here = (here[:, None] == lax.iota(jnp.int32, front)[None, :]).astype(BF)
        grad = mm(mid_grad[:, 0, :], hot_here)
        placed = placed - jnp.where(jnp.arange(nmid)[:, None, None] == ix, grad[None], 0.0)

    with jax.named_scope("contrib_sum"):
        s = half_sum(placed, flip).astype(BF)
        s = s.reshape(nx, hk, nc, ny, zi).transpose(3, 0, 1, 2, 4).reshape(ny * nx, hk, width)
        ysx = ahead(leaf_yb, "x")
        y_all = jnp.stack([lax.select_n((k - ix) % nx, *ysx) for k in range(nx)])
        at = place(mid_map, iy).reshape(-1, 1, 256)
        s_own = jnp.sum(a2a(s, ("y", "x")).astype(F32), 0).astype(BF)
        s_own, y_all, at = lax.optimization_barrier((s_own, y_all, at))
        s = jnp.sum(spread(s_own, "z").astype(F32), 0)
        contrib = s.astype(BF)
        cpl_all = lax.all_gather(after(leaf_cpl, s_own), "x", axis=0)

    with jax.named_scope("gather"):
        w0 = after(wide, contrib)
        w1 = swap(w0)
        def part_of(i):
            return pl.BlockSpec((nz, rows, front), lambda *_: (0, i, 0))

        tile = 256

        rsel0 = pl.pallas_call(
            select_kernel,
            grid=(nmid * ncpl // tile,),
            in_specs=[pl.BlockSpec((1, 1, tile), lambda i: (i, 0, 0)), part_of(2)],
            out_specs=pl.BlockSpec((tile, blk), lambda i: (i, 0)),
            out_shape=jax.ShapeDtypeStruct((nmid * ncpl, blk), BF),
            compiler_params=PARAMS,
            name="root_select",
        )(at, w0)
        contrib = after(contrib, rsel0)
        rsel1 = swap(rsel0)

    def whole(shape):
        return pl.BlockSpec(shape, lambda *_: (0,) * len(shape))

    with jax.named_scope("mid_forward"):
        part_y, u = pl.pallas_call(
            mid_kernel,
            grid=(1,),
            in_specs=[SM, whole((hk, width)), part_of(0), part_of(0), part_of(1), part_of(1)],
            out_specs=[whole((hk, front)), whole((ny * nx, hk, ncpl))],
            out_shape=[
                jax.ShapeDtypeStruct((hk, front), BF),
                jax.ShapeDtypeStruct((ny * nx, hk, ncpl), BF),
            ],
            compiler_params=pltpu.CompilerParams(vmem_limit_bytes=40 * 2**20),
            name="mid_forward",
        )(core, contrib, w0, w1, w0, w1)
        pre = jnp.sum(after(w0, part_y, rsel1)[:, 3 * rows :].astype(F32), 0)
        pre = half_sum(jnp.concatenate(jnp.split(pre, g, 1), 0))
        u = a2a(u, ("y", "x"))

    with jax.named_scope("root"):
        root_y, coupled = pl.pallas_call(
            functools.partial(root_kernel, nx),
            in_specs=[VM] * 6,
            out_specs=[VM] * 2,
            out_shape=[
                jax.ShapeDtypeStruct((hk, blk), BF),
                jax.ShapeDtypeStruct((nx, hk, ncpl + 128), BF),
            ],
            compiler_params=PARAMS,
            name="root",
        )(u, rsel0, rsel1, pre, rinv_x, rinv_o)
        ys = ahead(after(part_y, root_y), "y")
        coupled = a2a(coupled, "x")

    with jax.named_scope("mid_backward"):
        mx = pl.pallas_call(
            back_kernel,
            grid=(1,),
            in_specs=[SM, whole((nx, hk, ncpl + 128))]
            + [whole((hk, front))] * ny
            + [part_of(0), part_of(0), part_of(1), part_of(1)],
            out_specs=whole((ny * nx, hk, width)),
            out_shape=jax.ShapeDtypeStruct((ny * nx, hk, width), BF),
            compiler_params=PARAMS,
            name="mid_backward",
        )(core, coupled, *ys, w0, w1, w0, w1)
        rx = jnp.sum(coupled[:, :, ncpl : ncpl + nc * rows].astype(F32), 0)
        alive = lax.iota(jnp.int32, order)[None, :] < leaf_size[:, None]
        inv_m = jnp.where(alive[:, None, :], after(leaf_inv, root_y), 0)
        nmat = jnp.einsum(
            "lpxq,xlqc->lpc",
            inv_m.reshape(nl, share, nx, share),
            after(cpl_all, mx),
            preferred_element_type=F32,
        ).astype(BF)
        base = jnp.einsum("xlkq,lpxq->lkp", y_all, inv4, preferred_element_type=F32)
        mx = after(a2a(mx, ("y", "x")), nmat, base).reshape(ny, nx, hk, nc, zi)
        mx = mx.transpose(1, 2, 3, 0, 4).reshape(nx, hk, front)
        mo = swap(mx)

    with jax.named_scope("leaf_backward"):
        leaf_x = pl.pallas_call(
            leaf_kernel,
            grid_spec=pltpu.PrefetchScalarGridSpec(
                num_scalar_prefetch=2,
                grid=(nl,),
                in_specs=[
                    pl.BlockSpec((1, hk, front), lambda i, parent, *_: (parent[i], 0, 0)),
                    pl.BlockSpec((1, hk, front), lambda i, parent, *_: (parent[i], 0, 0)),
                    pl.BlockSpec((1, 1, ncpl), lambda i, *_: (i, 0, 0)),
                    pl.BlockSpec((1, share, ncpl), lambda i, *_: (i, 0, 0)),
                    pl.BlockSpec((1, nk, share), lambda i, *_: (i, 0, 0)),
                ],
                out_specs=pl.BlockSpec((1, nk, share), lambda i, *_: (i, 0, 0)),
            ),
            out_shape=jax.ShapeDtypeStruct((nl, nk, share), F32),
            compiler_params=PARAMS,
            name="leaf_backward",
        )(leaf_parent, core, mx, mo, target[:, None, :], nmat, base)

    with jax.named_scope("outputs"):

        def mine_of(v, at):
            v = lax.dynamic_index_in_dim(v, ix, 0, keepdims=False)
            return lax.dynamic_slice(v, (0, at), (hk, rows))

        om = mine_of(mx, own), mine_of(mo, half + own)
        out_m = jnp.concatenate([pick(*om), pick(om[1], om[0])], 0)
        ro = swap(rx[:, rows:])
        out_r = jnp.concatenate(
            [pick(rx[:, :rows], ro), pick(ro, rx[:, :rows])], 0
        )
    return leaf_x, out_m.astype(F32)[:, None, :], out_r


def solution(mesh):
    grid = Mesh(mesh.devices.reshape(4, 8, 2, 4), ("y", "z", "c", "x"))
    row = ("y", "z", "c")
    placed = (
        P(row, None, "x"),
        P(row, "x", None),
        P(row, "x", None),
        P(row),
        P(row),
        P(row, None),
        P(None, "x", row),
        P("x", row, None),
        P("x", row, None),
        P(),
        P(None, row),
        P(row, None),
    )
    return jax.shard_map(
        body,
        mesh=grid,
        in_specs=placed,
        out_specs=(P(row, None, "x"), P(None, "x", row), P(None, row)),
        check_vma=False,
    )
```

```python
import functools

import jax
import jax.numpy as jnp
from jax import lax
from jax.experimental import pallas as pl
from jax.experimental.pallas import tpu as pltpu
from jax.sharding import Mesh, PartitionSpec as P

BF = jnp.bfloat16
F32 = jnp.float32
VM = pl.BlockSpec(memory_space=pltpu.VMEM)
SM = pl.BlockSpec(memory_space=pltpu.SMEM)
PARAMS = pltpu.CompilerParams(vmem_limit_bytes=60 * 2**20)


def mm(a, b):
    return jnp.dot(a, b, preferred_element_type=F32)


def mm_t(a, b):
    return lax.dot_general(a, b, (((1,), (1,)), ((), ())), preferred_element_type=F32)


def a2a(v, axes):
    return lax.all_to_all(v, axes, 0, 0, tiled=True)


def spread(v, axes):
    n = lax.axis_size(axes)
    return a2a(jnp.broadcast_to(v[None], (n,) + v.shape), axes)


def swap(v):
    return lax.ppermute(v, "c", [(0, 1), (1, 0)])


def ahead(v, axis):
    n = lax.axis_size(axis)
    return [v] + [
        lax.ppermute(v, axis, [((i + k) % n, i) for i in range(n)]) for k in range(1, n)
    ]


def flip(v):
    n = v.shape[-1] // 2
    return jnp.concatenate([v[..., n:], v[..., :n]], -1)


def after(v, *first):
    return lax.optimization_barrier((v,) + first)[0]


def by_core(core, first, second):
    return jnp.where(core == 0, first, second), jnp.where(core == 0, second, first)


def root_pack_kernel(at, inv_ref, grad_ref, cpl_ref, out_ref, keep_ref):
    rows, nk = inv_ref.shape[0], grad_ref.shape[0]
    keep_ref[...] = inv_ref[...]
    out_ref[:rows, :] = inv_ref[...]
    out_ref[rows : rows + nk, :] = mm(grad_ref[...], inv_ref[...]).astype(BF)
    out_ref[rows + nk :, :] = cpl_ref[...]


def pack_kernel(nk, iy, inv_ref, g0, g1, g2, g3, out_ref):
    rows, front = inv_ref.shape
    got = (g0, g1, g2, g3)
    n = g0.shape[1]
    lane = lax.broadcasted_iota(jnp.int32, (rows, 128), 1) // 32
    for pair in range(front // 256):
        a = inv_ref[:, pair * 256 : pair * 256 + 128].astype(F32)
        b = inv_ref[:, pair * 256 + 128 : pair * 256 + 256].astype(F32)
        for c in range(2):
            if c == 0:
                parts = [a, pltpu.roll(a, 96, 1), pltpu.roll(b, 64, 1), pltpu.roll(b, 32, 1)]
            else:
                parts = [pltpu.roll(a, 96, 1), pltpu.roll(a, 64, 1), pltpu.roll(b, 32, 1), b]
            v = jnp.where(
                lane == 0,
                parts[0],
                jnp.where(lane == 1, parts[1], jnp.where(lane == 2, parts[2], parts[3])),
            )
            at = c * (front // 2) + pair * 128
            out_ref[:rows, at : at + 128] = v.astype(BF)
    for i, ref in enumerate(got):
        out_ref[2 * rows : 3 * rows, i * n : (i + 1) * n] = ref[:rows, :]
        s = lax.rem(iy[0] + i, len(got))
        for j in range(len(got)):

            @pl.when(s == j)
            def _():
                out_ref[rows : 2 * rows, j * n : (j + 1) * n] = ref[rows + nk :, :]

    pre = sum(ref[rows : rows + nk, :].astype(F32) for ref in got).astype(BF)
    step = nk // len(got)
    for i in range(len(got)):
        out_ref[3 * rows :, i * n : (i + 1) * n] = pre[i * step : (i + 1) * step, :]


def mid_kernel(core, h_ref, m0_ref, m1_ref, c0_ref, c1_ref, y_ref, u_ref):
    nz, rows, front = m0_ref.shape
    zi, ncpl = nz * rows, u_ref.shape[-1]
    m0 = m0_ref[...].reshape(zi, front)
    m1 = m1_ref[...].reshape(zi, front)
    y = -(mm(h_ref[:, :zi], m0) + mm(h_ref[:, zi:], m1))
    y = y.astype(BF)
    y_ref[...] = y
    mine, other = by_core(core[0], y[:, : front // 2], y[:, front // 2 :])
    u = jnp.zeros(u_ref.shape[1:], F32)
    for half, ref in ((mine, c0_ref), (other, c1_ref)):
        for i in range(front // ncpl):
            block = ref[:, :, i * ncpl : (i + 1) * ncpl].reshape(zi, ncpl)
            u += mm(half[:, i * zi : (i + 1) * zi], block)
    u_ref[...] = jnp.broadcast_to(u.astype(BF)[None], u_ref.shape)


def select_kernel(at_ref, w_ref, out_ref):
    nz, rows, front = w_ref.shape
    zi, tile = nz * rows, out_ref.shape[0]
    ncol = out_ref.shape[1]
    at = jnp.broadcast_to(at_ref[0], (zi, tile)).T
    lane = lax.broadcasted_iota(jnp.int32, (tile, zi), 1)
    acc = jnp.zeros(out_ref.shape, F32)
    for i in range(front // ncol):
        hot = jnp.where(at - i * zi == lane, 1.0, 0.0).astype(BF)
        acc += mm(hot, w_ref[:, :, i * ncol : (i + 1) * ncol].reshape(zi, ncol))
    out_ref[...] = acc.astype(BF)


def root_kernel(nx, u_ref, r0_ref, r1_ref, pre_ref, w0_ref, w1_ref, y_ref, cpl_ref):
    n = u_ref.shape[-1]
    acc = pre_ref[...]
    sel = []
    for x in range(nx):
        u = sum(u_ref[j].astype(F32) for j in range(x, u_ref.shape[0], nx))
        sel.append(r0_ref[x * n : (x + 1) * n, :] + r1_ref[x * n : (x + 1) * n, :])
        acc -= mm(u.astype(BF), sel[x])
    y = acc.astype(BF)
    y_ref[...] = y
    both = jnp.concatenate([w0_ref[...], w1_ref[...]], 0)
    both = jnp.concatenate([both, jnp.zeros((128 - both.shape[0], both.shape[1]), BF)], 0)
    part = mm_t(y, both).astype(BF)
    for x in range(nx):
        cpl_ref[x, :, :n] = mm_t(y, sel[x]).astype(BF)
        cpl_ref[x, :, n:] = part


def back_kernel(core, cp_ref, y0, y1, y2, y3, m0_ref, m1_ref, c0_ref, c1_ref, out_ref):
    nz, rows, front = m0_ref.shape
    zi, ncpl = nz * rows, cp_ref.shape[-1] - 128
    cp = sum(cp_ref[j, :, :ncpl].astype(F32) for j in range(cp_ref.shape[0])).astype(BF)
    halves = []
    for ref in (c0_ref, c1_ref):
        parts = [
            mm_t(cp, ref[:, :, i * ncpl : (i + 1) * ncpl].reshape(zi, ncpl))
            for i in range(front // ncpl)
        ]
        halves.append(jnp.concatenate(parts, 1))
    full = jnp.concatenate(by_core(core[0], halves[0], halves[1]), 1)
    y = sum(r[...].astype(F32) for r in (y0, y1, y2, y3))
    w = (y - full).astype(BF)
    x0 = mm_t(w, m0_ref[...].reshape(zi, front))
    x1 = mm_t(w, m1_ref[...].reshape(zi, front))
    x = jnp.concatenate([x0, x1], 1).astype(BF)
    out_ref[...] = jnp.broadcast_to(x[None], out_ref.shape)


def leaf_kernel(parent, core, x0_ref, x1_ref, at_ref, n_ref, base_ref, out_ref):
    half = x0_ref.shape[2] // 2
    ncpl, chunk = at_ref.shape[2], 256
    x1 = jnp.concatenate([x1_ref[0, :, half:], x1_ref[0, :, :half]], 1)
    x = jnp.concatenate(by_core(core[0], x0_ref[0], x1), 0)
    at = at_ref[0]
    place = lax.broadcasted_iota(jnp.int32, (chunk, ncpl), 0)
    acc = jnp.zeros((x.shape[0], ncpl), F32)
    for i in range(x.shape[1] // chunk):
        hot = jnp.where(at - i * chunk == place, 1.0, 0.0).astype(BF)
        acc += mm(x[:, i * chunk : (i + 1) * chunk], hot)
    out_ref[0] = base_ref[0] - mm_t(acc.astype(BF), n_ref[0])


def body(
    leaf_grad,
    leaf_inv,
    leaf_cpl,
    leaf_size,
    leaf_parent,
    leaf_map,
    mid_grad,
    mid_inv,
    mid_cpl,
    mid_map,
    root_grad,
    root_inv,
):
    ny, nz, nc, nx = (lax.axis_size(a) for a in ("y", "z", "c", "x"))
    iy, iz, ic, ix = (lax.axis_index(a) for a in ("y", "z", "c", "x"))
    nl, share, order = leaf_inv.shape
    nk = leaf_grad.shape[1]
    hk = nk // nc
    rows, front = mid_inv.shape[1:]
    ncpl = leaf_cpl.shape[2]
    nmid = mid_map.shape[0]
    zi = nz * rows
    half = front // nc
    width = front // ny
    blk = front // nx
    core = ic.astype(jnp.int32).reshape(1)

    def pick(first, second):
        return jnp.where(ic == 0, first, second)

    def place(m, y0):
        c = (m // rows % nc) ^ ic
        z = m // (rows * nc) % nz
        y = (m // (rows * nc * nz) - y0) % ny
        return (c * ny + y) * zi + z * rows + m % rows

    def half_sum(v, turn=lambda t: t):
        lo, hi = v[..., :hk, :], v[..., hk:, :]
        return pick(lo, hi) + swap(turn(pick(hi, lo).astype(BF))).astype(F32)

    own = iy * zi + iz * rows

    with jax.named_scope("leaf_forward"):
        live = (ix * share + lax.iota(jnp.int32, share))[None, :] < leaf_size[:, None]
        live = live[:, None, :]
        inv4 = leaf_inv.reshape(nl, share, nx, share)
        part = jnp.einsum(
            "lkp,lpxq->xlkq", leaf_grad, inv4, preferred_element_type=F32
        ).astype(BF)
        leaf_y = jnp.where(live, jnp.sum(a2a(part, "x").astype(F32), 0), 0.0)
        leaf_yb = leaf_y.astype(BF)

    with jax.named_scope("gather"):
        place_x = ix.astype(jnp.int32).reshape(1)
        mine, rinv_x = pl.pallas_call(
            root_pack_kernel,
            grid_spec=pltpu.PrefetchScalarGridSpec(
                num_scalar_prefetch=1,
                grid=(1,),
                in_specs=[
                    pl.BlockSpec((rows, blk), lambda i, at: (0, at[0])),
                    pl.BlockSpec((nk, rows), lambda i, at: (0, 0)),
                    pl.BlockSpec((rows, ncpl), lambda i, at: (0, 0)),
                ],
                out_specs=[
                    pl.BlockSpec((2 * rows + nk, blk), lambda i, at: (0, 0)),
                    pl.BlockSpec((rows, blk), lambda i, at: (0, 0)),
                ],
            ),
            out_shape=[
                jax.ShapeDtypeStruct((2 * rows + nk, blk), BF),
                jax.ShapeDtypeStruct((rows, blk), BF),
            ],
            compiler_params=PARAMS,
            name="root_pack",
        )(place_x, root_inv, root_grad, mid_cpl[0])
        rinv_o = swap(rinv_x)
        got = ahead(mine, "y")
        g = front // blk
        payload = pl.pallas_call(
            functools.partial(pack_kernel, nk),
            in_specs=[SM] + [VM] * 5,
            out_specs=VM,
            out_shape=jax.ShapeDtypeStruct((3 * rows + nk // g, front), BF),
            compiler_params=PARAMS,
            name="pack",
        )(iy.astype(jnp.int32).reshape(1), after(mid_inv[0], part), *got)
        wide = lax.all_gather(payload, "z", axis=0)

    with jax.named_scope("leaf_spread"):
        target = place(leaf_map, 0)
        hot = (target[:, :, None] == lax.iota(jnp.int32, front)).astype(BF)
        cpl_wide = jnp.einsum(
            "lcn,lpc->lnp", hot, leaf_cpl, preferred_element_type=F32
        ).astype(BF)
        parent_of = jnp.arange(nmid)[:, None] == leaf_parent[None, :]
        lhs = jnp.where(parent_of[:, None, :, None], leaf_yb.transpose(1, 0, 2)[None], 0)
        placed = jnp.einsum(
            "mlp,lnp->mn",
            lhs.reshape(nmid * nk, nl, share),
            cpl_wide,
            preferred_element_type=F32,
        ).reshape(nmid, nk, front)
        here = own + lax.iota(jnp.int32, rows)
        hot_here = (here[:, None] == lax.iota(jnp.int32, front)[None, :]).astype(BF)
        grad = mm(mid_grad[:, 0, :], hot_here)
        placed = placed - jnp.where(jnp.arange(nmid)[:, None, None] == ix, grad[None], 0.0)

    with jax.named_scope("contrib_sum"):
        s = half_sum(placed, flip).astype(BF)
        s = s.reshape(nx, hk, nc, ny, zi).transpose(3, 0, 1, 2, 4).reshape(ny * nx, hk, width)
        ysx = ahead(leaf_yb, "x")
        y_all = jnp.stack([lax.select_n((k - ix) % nx, *ysx) for k in range(nx)])
        at = place(mid_map, iy).reshape(-1, 1, 256)
        s_own = jnp.sum(a2a(s, ("y", "x")).astype(F32), 0).astype(BF)
        s_own, y_all, at = lax.optimization_barrier((s_own, y_all, at))
        s = jnp.sum(spread(s_own, "z").astype(F32), 0)
        contrib = s.astype(BF)
        cpl_all = lax.all_gather(after(leaf_cpl, s_own), "x", axis=0)

    with jax.named_scope("gather"):
        w0 = after(wide, contrib)
        w1 = swap(w0)
        def part_of(i):
            return pl.BlockSpec((nz, rows, front), lambda *_: (0, i, 0))

        tile = 256

        rsel0 = pl.pallas_call(
            select_kernel,
            grid=(nmid * ncpl // tile,),
            in_specs=[pl.BlockSpec((1, 1, tile), lambda i: (i, 0, 0)), part_of(2)],
            out_specs=pl.BlockSpec((tile, blk), lambda i: (i, 0)),
            out_shape=jax.ShapeDtypeStruct((nmid * ncpl, blk), BF),
            compiler_params=PARAMS,
            name="root_select",
        )(at, w0)
        contrib = after(contrib, rsel0)
        rsel1 = swap(rsel0)

    def whole(shape):
        return pl.BlockSpec(shape, lambda *_: (0,) * len(shape))

    with jax.named_scope("mid_forward"):
        part_y, u = pl.pallas_call(
            mid_kernel,
            grid=(1,),
            in_specs=[SM, whole((hk, width)), part_of(0), part_of(0), part_of(1), part_of(1)],
            out_specs=[whole((hk, front)), whole((ny * nx, hk, ncpl))],
            out_shape=[
                jax.ShapeDtypeStruct((hk, front), BF),
                jax.ShapeDtypeStruct((ny * nx, hk, ncpl), BF),
            ],
            compiler_params=pltpu.CompilerParams(vmem_limit_bytes=40 * 2**20),
            name="mid_forward",
        )(core, contrib, w0, w1, w0, w1)
        pre = jnp.sum(after(w0, part_y, rsel1)[:, 3 * rows :].astype(F32), 0)
        pre = half_sum(jnp.concatenate(jnp.split(pre, g, 1), 0))
        u = a2a(u, ("y", "x"))

    with jax.named_scope("root"):
        root_y, coupled = pl.pallas_call(
            functools.partial(root_kernel, nx),
            in_specs=[VM] * 6,
            out_specs=[VM] * 2,
            out_shape=[
                jax.ShapeDtypeStruct((hk, blk), BF),
                jax.ShapeDtypeStruct((nx, hk, ncpl + 128), BF),
            ],
            compiler_params=PARAMS,
            name="root",
        )(u, rsel0, rsel1, pre, rinv_x, rinv_o)
        ys = ahead(after(part_y, root_y), "y")
        coupled = a2a(coupled, "x")

    with jax.named_scope("mid_backward"):
        mx = pl.pallas_call(
            back_kernel,
            grid=(1,),
            in_specs=[SM, whole((nx, hk, ncpl + 128))]
            + [whole((hk, front))] * ny
            + [part_of(0), part_of(0), part_of(1), part_of(1)],
            out_specs=whole((ny * nx, hk, width)),
            out_shape=jax.ShapeDtypeStruct((ny * nx, hk, width), BF),
            compiler_params=PARAMS,
            name="mid_backward",
        )(core, coupled, *ys, w0, w1, w0, w1)
        rx = jnp.sum(coupled[:, :, ncpl : ncpl + nc * rows].astype(F32), 0)
        alive = lax.iota(jnp.int32, order)[None, :] < after(leaf_size, root_y)[:, None]
        inv_m = jnp.where(alive[:, None, :], after(leaf_inv, root_y), 0)
        nmat = jnp.einsum(
            "lpxq,xlqc->lpc",
            inv_m.reshape(nl, share, nx, share),
            after(cpl_all, mx),
            preferred_element_type=F32,
        ).astype(BF)
        base = jnp.einsum("xlkq,lpxq->lkp", y_all, inv4, preferred_element_type=F32)
        mx = after(a2a(mx, ("y", "x")), nmat, base).reshape(ny, nx, hk, nc, zi)
        mx = mx.transpose(1, 2, 3, 0, 4).reshape(nx, hk, front)
        mo = swap(mx)

    with jax.named_scope("leaf_backward"):
        leaf_x = pl.pallas_call(
            leaf_kernel,
            grid_spec=pltpu.PrefetchScalarGridSpec(
                num_scalar_prefetch=2,
                grid=(nl,),
                in_specs=[
                    pl.BlockSpec((1, hk, front), lambda i, parent, *_: (parent[i], 0, 0)),
                    pl.BlockSpec((1, hk, front), lambda i, parent, *_: (parent[i], 0, 0)),
                    pl.BlockSpec((1, 1, ncpl), lambda i, *_: (i, 0, 0)),
                    pl.BlockSpec((1, share, ncpl), lambda i, *_: (i, 0, 0)),
                    pl.BlockSpec((1, nk, share), lambda i, *_: (i, 0, 0)),
                ],
                out_specs=pl.BlockSpec((1, nk, share), lambda i, *_: (i, 0, 0)),
            ),
            out_shape=jax.ShapeDtypeStruct((nl, nk, share), F32),
            compiler_params=pltpu.CompilerParams(vmem_limit_bytes=40 * 2**20),
            name="leaf_backward",
        )(leaf_parent, core, mx, mo, after(target, root_y)[:, None, :], nmat, base)

    with jax.named_scope("outputs"):

        def mine_of(v, at):
            v = lax.dynamic_index_in_dim(v, ix, 0, keepdims=False)
            return lax.dynamic_slice(v, (0, at), (hk, rows))

        om = mine_of(mx, own), mine_of(mo, half + own)
        out_m = jnp.concatenate([pick(*om), pick(om[1], om[0])], 0)
        ro = swap(rx[:, rows:])
        out_r = jnp.concatenate(
            [pick(rx[:, :rows], ro), pick(ro, rx[:, :rows])], 0
        )
    return leaf_x, out_m.astype(F32)[:, None, :], out_r


def solution(mesh):
    grid = Mesh(mesh.devices.reshape(4, 8, 2, 4), ("y", "z", "c", "x"))
    row = ("y", "z", "c")
    placed = (
        P(row, None, "x"),
        P(row, "x", None),
        P(row, "x", None),
        P(row),
        P(row),
        P(row, None),
        P(None, "x", row),
        P("x", row, None),
        P("x", row, None),
        P(),
        P(None, row),
        P(row, None),
    )
    return jax.shard_map(
        body,
        mesh=grid,
        in_specs=placed,
        out_specs=(P(row, None, "x"), P(None, "x", row), P(None, row)),
        check_vma=False,
    )
```
